32 devices in a mesh: wide: 8 (over y, x, core), blk: 4 (over z).
Axes of the slice: x: 2, y: 2, z: 4, core: 2. Of those that a mesh axis runs over, the one named last changes fastest.
Arguments:
- audio: bfloat16 [4096, 1024], P(('wide', 'blk')), may hold values from -1 to 1
- video: bfloat16 [4096, 1024], P(('wide', 'blk')), may hold values from -1 to 1
- owner: int32 [4096, 1], P(('wide', 'blk')), may hold values from 0 to 7; in each aligned block of 128 rows (0 to 127, 128 to 255, ...) at most 32 rows name the same one
- clip_feats: bfloat16 [8192, 1024], P(('wide', 'blk')), may hold values from -24 to 24
- lengths: int32 [8192], P(('wide', 'blk')), may hold values from 1 to 16
- proj_weight: bfloat16 [1024, 1024], replicated, may hold values from -0.1875 to 0.1875
Outputs:
- audio_grad: bfloat16 [4096, 1024], P(('wide', 'blk'))
- feats_grad: bfloat16 [8192, 1024], P(('wide', 'blk'))
- weight_grad: float32 [1024, 1024], P('wide')
The draws below stay inside these ranges and needn't reach their ends.
Inputs may be any that keep to these rules, and one draw needn't show every extreme that they name: Among the 128 rows of one device, no owner is named more than 32 times, a bound that some block reaches.
All inputs are finite; a program needn't handle non-finite values.
Results may differ from the reference program's by a relative error of at most 0.02.
Values may be sent and summed in bfloat16 or wider, within the bound.
A program may use at most 64 MiB of HBM per device.

```python
import math
from functools import partial
import jax
import jax.numpy as jnp
import numpy as np
from jax import lax

EMBED = 1024
CLIPS_DEV = 128
CAP = 32
ROWS = 4096
SLOTS_ALL = 8192
N_WIDE = 8
N_BLK = 4


def plant(entries, key, low, largest):
    shape = entries.shape
    index_at = [jax.random.randint(jax.random.fold_in(key, axis), (), 0, shape[axis]) for axis in range(len(shape))]
    entries = entries.at[tuple(index_at)].set(low)
    longest = shape.index(max(shape))
    index_at[longest] = (index_at[longest] + 1) % shape[longest]
    return entries.at[tuple(index_at)].set(largest)


def raised(drawn, rng, source, target, blocks, factor):
    owner, partner = [(jnp.arange(drawn.shape[dim]) // (drawn.shape[dim] // blocks)).reshape([-1 if axis == dim else 1 for axis in range(drawn.ndim)]) for dim in (source, target)]
    chosen = jax.random.permutation(rng, blocks)[partner]
    strong = (owner == chosen) | (owner == (partner + blocks // 2) % blocks)
    return jnp.where(strong, factor * drawn, drawn)


def level_of(stream_key, extent, pieces, least, high):
    factor_of = 1.0
    for axis_at, parts in pieces:
        heights = jax.random.uniform(jax.random.fold_in(jax.random.fold_in(stream_key, 6), axis_at), (parts,), jnp.float32, least / len(pieces), high / len(pieces))
        factor_of = factor_of * jnp.repeat(jnp.exp(heights), extent[axis_at] // parts).reshape((-1,) + (1,) * (len(extent) - 1 - axis_at))
    return factor_of


def routed_block(stream_key, own, number, rows, amount, top, bound, lean):
    sequence = jax.random.permutation(stream_key, amount)
    packed, ordinary = portions_of(amount, rows * top, bound, lean, True), portions_of(amount, rows * top, bound, lean, False)
    places = jnp.arange(amount)

    def named(sizes, turn):
        used = int((sizes > 0).sum())
        fixed = max(1, used // 4)
        passed = fixed + (places - fixed + turn * (used - fixed)) % max(1, amount - fixed)
        return jnp.zeros((amount,), jnp.int32).at[sequence[jnp.where(places < fixed, places, passed)]].set(jnp.asarray(sizes, jnp.int32))

    sizes = jnp.where(number % 4 == 0, named(packed, number // 4), named(ordinary, number - number // 4 - 1))
    mixed = jax.random.permutation(jax.random.fold_in(own, 3), amount)
    source_of, sink = mixed[0:amount // 2 * 2:2], mixed[1:amount // 2 * 2:2]
    room = jnp.minimum(sizes[source_of] - 1, bound - sizes[sink]) // 2
    room = jnp.where((source_of == sequence[0]) | (sink == sequence[0]) | (sizes[sink] == 0), 0, jnp.maximum(room, 0))
    passed = jax.random.randint(jax.random.fold_in(own, 4), (amount // 2,), 0, 1 << 20) % (room + 1)
    sizes = sizes.at[source_of].add(-passed).at[sink].add(passed)
    items = jnp.searchsorted(jnp.cumsum(sizes), jnp.arange(rows * top), side="right").astype(jnp.int32)
    grid = items.reshape(top, rows).T
    grid = grid[jax.random.permutation(jax.random.fold_in(own, 1), rows)]
    turn = jax.random.randint(jax.random.fold_in(own, 2), (rows, 1), 0, top)
    return jnp.take_along_axis(grid, (jnp.arange(top)[None, :] + turn) % top, axis=1)


def portions_of(amount, total, bound, lean, full):
    weights = [(1 << 20) // math.isqrt(rank ** lean) + 1 for rank in range(1, amount + 1)]
    largest = bound if full else min(bound, max(-(-total // amount), total * weights[0] // sum(weights)))
    least = 1 if total - largest >= amount - 1 else 0
    counts, rest = [largest] + [least] * (amount - 1), total - largest - least * (amount - 1)
    while rest > 0:
        free = [i for i in range(1, amount) if counts[i] < largest] or [i for i in range(1, amount) if counts[i] < bound]
        mass, budget = sum([weights[i] for i in free]), rest
        for i in free:
            more = min(bound - counts[i], max(1, budget * weights[i] // mass), rest)
            counts[i] = counts[i] + more
            rest = rest - more
    return np.array(counts)


def scatter_about(stream_key, shape, width, bound, shards=(), kind=jnp.bfloat16):
    entries = jax.random.normal(stream_key, shape, jnp.float32) * width
    if len(shards) > 0:
        entries = level_of(stream_key, shape, shards, -0.22, 0.18) * entries
    return jnp.clip(entries, min=-bound, max=bound).astype(kind)


def bell_draw_with(rng, shape, scale, limit, split, heavy, held_as=jnp.bfloat16):
    drawn = scale * jax.random.normal(rng, shape, jnp.float32)
    if split:
        drawn = drawn * level_of(rng, shape, split, -0.22, 0.18)
    return jnp.clip(raised(drawn, jax.random.fold_in(rng, 3), *heavy), -limit, limit).astype(held_as)


def setup_inputs(seed: int = 0) -> dict:
    streams_of = jax.random.split(jax.random.key(seed), 7)
    audio = scatter_about(streams_of[0], (ROWS, EMBED), 0.177, 1.0, ((0, 32),))
    video = scatter_about(streams_of[1], (ROWS, EMBED), 0.177, 1.0, ((0, 32),))
    owner_keys = jax.random.split(jax.random.fold_in(streams_of[2], 1), ROWS // CLIPS_DEV)
    owner_turns = jax.random.permutation(jax.random.fold_in(streams_of[2], 3), ROWS // CLIPS_DEV)
    owner = jax.vmap(lambda own, number: routed_block(jax.random.fold_in(streams_of[2], 2), own, number, CLIPS_DEV, N_WIDE, 1, CAP, 2))(owner_keys, owner_turns).reshape((ROWS, 1))
    clip_feats = bell_draw_with(streams_of[3], (SLOTS_ALL, EMBED), 2.0, 24.0, ((0, 32),), (0, 1, 32, 2.75))
    lengths = plant(jax.random.randint(streams_of[4], (SLOTS_ALL,), 1, 17), jax.random.fold_in(streams_of[4], 1), 1, 16).astype(jnp.int32)
    proj_weight = scatter_about(streams_of[5], (EMBED, EMBED), EMBED ** -0.5, 0.1875)
    return dict(audio=audio, video=video, owner=owner, clip_feats=clip_feats, lengths=lengths, proj_weight=proj_weight)


def group_grads(group_pair):
    audio_g, video_g = group_pair
    scores = jnp.dot(audio_g, video_g.T, preferred_element_type=jnp.float32)
    pair_count = audio_g.shape[0]
    labels = (jnp.arange(pair_count, dtype=jnp.int32)[:, None] == jnp.arange(pair_count, dtype=jnp.int32)[None, :]).astype(jnp.float32)
    coeffs = (4.0 / N_BLK * (jax.nn.sigmoid(4.0 * scores - 2.0) - labels)).astype(jnp.bfloat16)
    audio_part = jnp.dot(coeffs, video_g, preferred_element_type=jnp.float32).astype(jnp.bfloat16)
    video_part = jnp.dot(coeffs.T, audio_g, preferred_element_type=jnp.float32).astype(jnp.bfloat16)
    return (audio_part, video_part)

def reference(audio, video, owner, clip_feats, lengths, proj_weight):
    audio_groups = audio.reshape(N_WIDE, N_BLK * CLIPS_DEV, EMBED)
    video_groups = video.reshape(N_WIDE, N_BLK * CLIPS_DEV, EMBED)
    audio_grad, video_grad = lax.map(group_grads, (audio_groups, video_groups))
    audio_grad = audio_grad.reshape(ROWS, EMBED)
    owner_peer = owner.reshape(N_WIDE, N_BLK, CLIPS_DEV).astype(jnp.int32)
    onehot = (owner_peer[..., None] == jnp.arange(N_WIDE, dtype=jnp.int32)[None, None, None, :]).astype(jnp.int32)
    before = (jnp.cumsum(onehot, axis=2).astype(jnp.int32) - onehot) * onehot
    slot_rank = lax.optimization_barrier(jnp.sum(before, axis=3)).astype(jnp.int32)
    source = jnp.arange(N_WIDE, dtype=jnp.int32).reshape(N_WIDE, 1, 1)
    group_pos = jnp.arange(N_BLK, dtype=jnp.int32).reshape(1, N_BLK, 1)
    target = (((owner_peer * N_BLK + group_pos) * N_WIDE + source) * CAP + slot_rank).astype(jnp.int32)
    received = jnp.zeros((SLOTS_ALL, EMBED), jnp.bfloat16)
    received = received.at[target.reshape(-1)].set(video_grad.reshape(ROWS, EMBED))
    length_scale = lax.rsqrt(lengths.astype(jnp.float32))[:, None]
    pooled = (clip_feats.astype(jnp.float32) * length_scale).astype(jnp.bfloat16)
    preact = jnp.dot(pooled, proj_weight, preferred_element_type=jnp.float32)
    _, pullback = jax.vjp(partial(jax.nn.gelu, approximate=False), preact)
    pre_grad = pullback(received.astype(jnp.float32))[0].astype(jnp.bfloat16)
    feats_grad = (jnp.dot(pre_grad, proj_weight.T, preferred_element_type=jnp.float32) * length_scale).astype(jnp.bfloat16)
    weight_grad = jnp.dot(pooled.T, pre_grad, preferred_element_type=jnp.float32)
    return (audio_grad, feats_grad, weight_grad)
```

```python
import functools

import jax
import jax.numpy as jnp
from jax import lax
from jax.experimental import pallas as pl
from jax.experimental.pallas import tpu as pltpu
from jax.sharding import PartitionSpec as P

F32 = jnp.float32
BF16 = jnp.bfloat16
TILE = 256
SPLIT = 2


def dot(a, b):
    return jnp.dot(a, b, preferred_element_type=F32)


def rows_dot(a, b):
    return lax.dot_general(a, b, (((1,), (1,)), ((), ())), preferred_element_type=F32)


def column_of(row):
    n = row.shape[1]
    diagonal = lax.broadcasted_iota(jnp.int32, (n, n), 0) == lax.broadcasted_iota(
        jnp.int32, (n, n), 1
    )
    return jnp.sum(jnp.where(diagonal, row, jnp.zeros_like(row)), axis=1, keepdims=True)


def kernel(
    nw, nb,
    audio, video, owner, lengths, feats_hbm, weight_hbm,
    audio_out, feats_out, weight_out,
    feats, weight, a_buf, v_buf, a_acc, v_acc, v_grad, scale, pooled, pooled_t, pooled_p,
    gate, packed, received, pre, pre_p, acc, snd, rcv, fin, zs, zr,
    local_sem, a_send, a_recv, v_send, v_recv, p_send, p_recv, x_send, x_recv,
    g_send, g_recv, r_send, r_recv, z_send, z_recv,
):
    w, k = lax.axis_index("wide"), lax.axis_index("blk")
    rows, width = audio.shape
    slots = feats.shape[0]
    cap = slots // nw
    block = width // nw
    half = width // 2
    n2 = nw // 2
    bits = n2.bit_length() - 1
    chunks, _, chunk = fin.shape
    per_half = chunks // 2
    factor = 4.0 / nb
    core = lax.rem(w, 2)
    partner = w + 1 - 2 * core
    mine = w // 2

    def remote(src, dst, send, recv, dw, dk):
        return pltpu.make_async_remote_copy(
            src_ref=src, dst_ref=dst, send_sem=send, recv_sem=recv,
            device_id=(dw, dk), device_id_type=pl.DeviceIdType.MESH,
        )

    w_copy = pltpu.make_async_copy(weight_hbm, weight, local_sem.at[0])
    f_copy = pltpu.make_async_copy(feats_hbm, feats, local_sem.at[1])
    f_copy.start()
    w_copy.start()

    barrier = pltpu.get_barrier_semaphore()

    def peer_of(d):
        return lax.rem(w + d, nw)

    @pl.loop(1, nw)
    def _(d):
        pl.semaphore_signal(
            barrier, inc=1, device_id=(peer_of(d), k), device_id_type=pl.DeviceIdType.MESH
        )

    @pl.when(k > 0)
    def _():
        pl.semaphore_signal(
            barrier, inc=1, device_id=(w, k - 1), device_id_type=pl.DeviceIdType.MESH
        )

    @pl.when(k < nb - 1)
    def _():
        pl.semaphore_signal(
            barrier, inc=1, device_id=(w, k + 1), device_id_type=pl.DeviceIdType.MESH
        )

    sides = jnp.where(k > 0, 1, 0) + jnp.where(k < nb - 1, 1, 0)
    pl.semaphore_wait(barrier, nw - 1 + sides)

    def hop(src, buf, send, recv, j, step):
        side = 0 if step > 0 else 1
        return remote(src, buf.at[j], send.at[side, j], recv.at[j], w, k + step)

    def forward(src, buf, send, recv, j, step):
        @pl.when((k < nb - 1) if step > 0 else (k > 0))
        def _():
            hop(src, buf, send, recv, j, step).start()

    def begin(own, buf, send, recv):
        forward(own, buf, send, recv, k, 1)
        forward(own, buf, send, recv, k, -1)

    def coeffs(scores, labels):
        return (factor * (jax.nn.sigmoid(4.0 * scores - 2.0) - labels)).astype(BF16)

    def add_block(own, other, total):
        total[...] += dot(coeffs(rows_dot(own[...], other[...]), 0.0), other[...])

    def relay(s, buf, send, recv, own, total):
        for step in (1, -1):
            j = k - step * s

            @pl.when((j >= 0) if step > 0 else (j <= nb - 1))
            def _():
                hop(buf.at[j], buf, send, recv, j, step).wait_recv()
                forward(buf.at[j], buf, send, recv, j, step)

        for step in (1, -1):
            j = k - step * s

            @pl.when((j >= 0) if step > 0 else (j <= nb - 1))
            def _():
                add_block(own, buf.at[j], total)

    def finish(own, buf, send, recv):
        for s in range(nb):
            for step in (1, -1):
                j = k - step * s

                @pl.when(
                    ((j >= 0) & (k < nb - 1)) if step > 0 else ((j <= nb - 1) & (k > 0))
                )
                def _():
                    hop(own if s == 0 else buf.at[j], buf, send, recv, j, step).wait_send()

    begin(audio, a_buf, a_send, a_recv)

    eye = (
        lax.broadcasted_iota(jnp.int32, (rows, rows), 0)
        == lax.broadcasted_iota(jnp.int32, (rows, rows), 1)
    ).astype(F32)
    v_acc[...] = dot(coeffs(rows_dot(video[...], audio[...]), eye), audio[...])
    a_acc[...] = dot(coeffs(rows_dot(audio[...], video[...]), eye), video[...])

    scale[...] = column_of(lax.rsqrt(lengths[...].astype(F32)))
    f_copy.wait()

    @pl.loop(0, width // TILE)
    def _(t):
        cols = pl.ds(pl.multiple_of(t * TILE, TILE), TILE)
        part = (feats[:, cols].astype(F32) * scale[...]).astype(BF16)
        pooled[:, cols] = part
        pooled_t[cols, :] = part.astype(F32).T.astype(BF16)

    def pooled_copy(i):
        other = 2 * i + 1 - core
        start = pl.multiple_of(other * block, block)
        return remote(
            pooled_t.at[pl.ds(start, block), :], pooled_p.at[i],
            p_send.at[i], p_recv.at[i], partner, k,
        )

    @pl.loop(0, n2)
    def _(i):
        pooled_copy(i).start()

    w_copy.wait()

    @pl.loop(0, width // TILE)
    def _(t):
        cols = pl.ds(pl.multiple_of(t * TILE, TILE), TILE)
        v = dot(pooled[...], weight[:, cols])
        cdf = 0.5 * (1.0 + lax.erf(v * (0.5**0.5)))
        density = jnp.exp(-0.5 * v * v) * 0.3989422804014327
        gate[:, cols] = cdf + v * density

    for s in range(1, nb):
        relay(s, a_buf, a_send, a_recv, video, v_acc)
        if s == max(1, nb - 2):
            begin(video, v_buf, v_send, v_recv)

    v_grad[...] = v_acc[...].astype(BF16)
    own_row = owner[...]
    own_col = column_of(own_row)
    earlier = lax.broadcasted_iota(jnp.int32, (rows, rows), 0) < lax.broadcasted_iota(
        jnp.int32, (rows, rows), 1
    )
    same = (own_col == own_row) & earlier
    rank = jnp.sum(jnp.where(same, 1, 0), axis=0, keepdims=True)
    target = own_row * cap + rank
    placing = (
        (lax.broadcasted_iota(jnp.int32, (slots, rows), 0) == target).astype(F32).astype(BF16)
    )
    for t in range(width // TILE):
        cols = slice(t * TILE, (t + 1) * TILE)
        placed = dot(placing, v_grad[:, cols])
        packed[:, :, cols] = placed.reshape(nw, cap, TILE).astype(BF16)

    def exchange(peer):
        return remote(
            packed.at[peer], received.at[w], x_send.at[peer], x_recv.at[w], peer, k
        )

    @pl.loop(1, nw)
    def _(d):
        exchange(peer_of(d)).start()

    received[w] = packed[w]

    relay(1, v_buf, v_send, v_recv, audio, a_acc)

    @pl.loop(1, nw)
    def _(d):
        peer = peer_of(d)
        remote(
            packed.at[peer], received.at[peer], x_send.at[peer], x_recv.at[peer], peer, k
        ).wait_recv()

    def grad_copy(h):
        return remote(pre.at[h], pre_p.at[h], g_send.at[h], g_recv.at[h], partner, k)

    for h in range(2):
        for t in range(half // TILE):
            lo = h * half + t * TILE
            cols = slice(lo, lo + TILE)
            grads = received[:, :, cols].astype(F32).reshape(slots, TILE)
            pre[h, :, t * TILE : (t + 1) * TILE] = (grads * gate[:, cols]).astype(BF16)
        grad_copy(h).start()

    @pl.loop(0, n2)
    def _(i):
        pooled_copy(i).wait_recv()

    def order(h):
        return list(range(bits)) if h == 0 else list(range(bits))[::-1]

    def index(h, t, flip, combo):
        taken = order(h)
        at = 0
        for place, bit in enumerate(taken):
            own = lax.rem(mine // (1 << bit), 2)
            if place < t:
                value = own
            elif place == t:
                value = 1 - own if flip else own
            else:
                value = (combo >> (place - t - 1)) & 1
            at = at + value * (1 << bit)
        return at

    def product(h, i):
        start = pl.multiple_of((2 * i + core) * block, block)
        return dot(pooled_t[pl.ds(start, block), :], pre[h]) + dot(pooled_p[i], pre_p[h])

    def scatter_copy(h, t, combo):
        bit = order(h)[t]
        sign = 1 - 2 * lax.rem(mine // (1 << bit), 2)
        peer = w + sign * (2 << bit)
        slot = n2 - (1 << (bits - t)) + combo
        return remote(
            snd.at[h, slot], rcv.at[h, slot], r_send.at[h, slot], r_recv.at[h, slot], peer, k
        )

    def combos(t):
        return range(1 << (bits - 1 - t))

    def slot_of(t, combo):
        return n2 - (1 << (bits - t)) + combo

    for h in range(2):
        grad_copy(h).wait_recv()
        for combo in combos(0):
            snd[h, slot_of(0, combo)] = product(h, index(h, 0, 1, combo)).astype(BF16)
            scatter_copy(h, 0, combo).start()
    for h in range(2):
        for combo in combos(0):
            i = index(h, 0, 0, combo)
            acc[h, i] = product(h, i)

    for s in range(2, nb - 1):
        relay(s, v_buf, v_send, v_recv, audio, a_acc)

    @pl.loop(0, width // TILE)
    def _(t):
        cols = pl.ds(pl.multiple_of(t * TILE, TILE), TILE)
        out = rows_dot(pre[0], weight[cols, :half]) + rows_dot(pre[1], weight[cols, half:])
        feats_out[:, cols] = (out * scale[...]).astype(BF16)

    for t in range(bits):
        for h in range(2):
            for combo in combos(t):
                scatter_copy(h, t, combo).wait_recv()
                i = index(h, t, 0, combo)
                acc[h, i] += rcv[h, slot_of(t, combo)].astype(F32)
            if t + 1 < bits:
                for combo in combos(t + 1):
                    i = index(h, t + 1, 1, combo)
                    snd[h, slot_of(t + 1, combo)] = acc[h, i].astype(BF16)
                    scatter_copy(h, t + 1, combo).start()

    for h in range(2):
        for q in range(per_half):
            fin[h * per_half + q] = acc[h, mine, :, q * chunk : (q + 1) * chunk]

    def sum_copy(side, q):
        return remote(
            zs.at[side, q], zr.at[side, q], z_send.at[side, q], z_recv.at[side, q],
            w, k + 1 - 2 * side,
        )

    @pl.loop(0, nb - 1 + chunks)
    def _(time):
        for side in range(2):
            place = k if side == 0 else nb - 1 - k
            q = time - place

            @pl.when((q >= 0) & (q < chunks))
            def _():
                @pl.when(place > 0)
                def _():
                    sum_copy(side, q).wait_recv()

                @pl.when(place < nb - 1)
                def _():
                    @pl.when(place > 0)
                    def _():
                        zs[side, q] = (fin[q] + zr[side, q].astype(F32)).astype(BF16)

                    @pl.when(place == 0)
                    def _():
                        zs[side, q] = fin[q].astype(BF16)

                    sum_copy(side, q).start()

    for q in range(chunks):
        cols = slice(q * chunk, (q + 1) * chunk)
        weight_out[:, cols] = fin[q]

        @pl.when(k > 0)
        def _():
            weight_out[:, cols] += zr[0, q].astype(F32)

        @pl.when(k < nb - 1)
        def _():
            weight_out[:, cols] += zr[1, q].astype(F32)

    for s in range(max(2, nb - 1), nb):
        relay(s, v_buf, v_send, v_recv, audio, a_acc)
    audio_out[...] = a_acc[...].astype(BF16)

    finish(audio, a_buf, a_send, a_recv)
    finish(video, v_buf, v_send, v_recv)

    @pl.loop(0, n2)
    def _(i):
        pooled_copy(i).wait_send()

    @pl.loop(1, nw)
    def _(d):
        exchange(peer_of(d)).wait_send()

    for h in range(2):
        grad_copy(h).wait_send()
        for t in range(bits):
            for combo in combos(t):
                scatter_copy(h, t, combo).wait_send()

    @pl.loop(0, chunks)
    def _(q):
        @pl.when(k < nb - 1)
        def _():
            sum_copy(0, q).wait_send()

        @pl.when(k > 0)
        def _():
            sum_copy(1, q).wait_send()


def shards(nw, nb, audio, video, owner, clip_feats, lengths, proj_weight):
    rows, width = audio.shape
    slots = clip_feats.shape[0]
    cap, block, half, n2 = slots // nw, width // nw, width // 2, nw // 2
    chunks = 2 * SPLIT
    chunk = width // chunks
    vmem = pl.BlockSpec(memory_space=pltpu.VMEM)
    hbm = pl.BlockSpec(memory_space=pl.ANY)
    dma = pltpu.SemaphoreType.DMA
    return pl.pallas_call(
        functools.partial(kernel, nw, nb),
        out_shape=(
            jax.ShapeDtypeStruct((rows, width), BF16),
            jax.ShapeDtypeStruct((slots, width), BF16),
            jax.ShapeDtypeStruct((block, width), F32),
        ),
        in_specs=[vmem, vmem, vmem, vmem, hbm, hbm],
        out_specs=(vmem, vmem, vmem),
        scratch_shapes=[
            pltpu.VMEM((slots, width), BF16),
            pltpu.VMEM(proj_weight.shape, BF16),
            pltpu.VMEM((nb, rows, width), BF16),
            pltpu.VMEM((nb, rows, width), BF16),
            pltpu.VMEM((rows, width), F32),
            pltpu.VMEM((rows, width), F32),
            pltpu.VMEM((rows, width), BF16),
            pltpu.VMEM((slots, 1), F32),
            pltpu.VMEM((slots, width), BF16),
            pltpu.VMEM((width, slots), BF16),
            pltpu.VMEM((n2, block, slots), BF16),
            pltpu.VMEM((slots, width), F32),
            pltpu.VMEM((nw, cap, width), BF16),
            pltpu.VMEM((nw, cap, width), BF16),
            pltpu.VMEM((2, slots, half), BF16),
            pltpu.VMEM((2, slots, half), BF16),
            pltpu.VMEM((2, n2, block, half), F32),
            pltpu.VMEM((2, n2, block, half), BF16),
            pltpu.VMEM((2, n2, block, half), BF16),
            pltpu.VMEM((chunks, block, chunk), F32),
            pltpu.VMEM((2, chunks, block, chunk), BF16),
            pltpu.VMEM((2, chunks, block, chunk), BF16),
            dma((2,)),
            dma((2, nb)), dma((nb,)),
            dma((2, nb)), dma((nb,)),
            dma((n2,)), dma((n2,)),
            dma((nw,)), dma((nw,)),
            dma((2,)), dma((2,)),
            dma((2, n2)), dma((2, n2)),
            dma((2, chunks)), dma((2, chunks)),
        ],
        compiler_params=pltpu.CompilerParams(
            collective_id=0, has_side_effects=True, vmem_limit_bytes=60 * 1024 * 1024
        ),
    )(
        audio, video, owner.reshape(1, rows), lengths.reshape(1, slots), clip_feats, proj_weight
    )


def solution(mesh):
    return jax.shard_map(
        functools.partial(shards, mesh.shape["wide"], mesh.shape["blk"]),
        mesh=mesh,
        in_specs=(
            P(("wide", "blk"), None),
            P(("wide", "blk"), None),
            P(("wide", "blk"), None),
            P(("wide", "blk"), None),
            P(("wide", "blk")),
            P(),
        ),
        out_specs=(P(("wide", "blk"), None), P(("wide", "blk"), None), P("wide", None)),
        check_vma=False,
    )
```

```python
import functools

import jax
import jax.numpy as jnp
from jax import lax
from jax.experimental import pallas as pl
from jax.experimental.pallas import tpu as pltpu
from jax.sharding import PartitionSpec as P

F32 = jnp.float32
BF16 = jnp.bfloat16
TILE = 256
SPLIT = 4


def dot(a, b):
    return jnp.dot(a, b, preferred_element_type=F32)


def rows_dot(a, b):
    return lax.dot_general(a, b, (((1,), (1,)), ((), ())), preferred_element_type=F32)


def column_of(row):
    n = row.shape[1]
    diagonal = lax.broadcasted_iota(jnp.int32, (n, n), 0) == lax.broadcasted_iota(
        jnp.int32, (n, n), 1
    )
    return jnp.sum(jnp.where(diagonal, row, jnp.zeros_like(row)), axis=1, keepdims=True)


def kernel(
    nw, nb,
    audio, video, owner, lengths, feats_hbm, weight_hbm,
    audio_out, feats_out, weight_out,
    feats, weight, a_buf, v_buf, a_acc, v_acc, v_grad, scale, pooled, pooled_t, pooled_p,
    gate, packed, received, pre, pre_p, acc, snd, rcv, fin, zs, zr,
    local_sem, a_send, a_recv, v_send, v_recv, p_send, p_recv, x_send, x_recv,
    g_send, g_recv, r_send, r_recv, z_send, z_recv,
):
    w, k = lax.axis_index("wide"), lax.axis_index("blk")
    rows, width = audio.shape
    slots = feats.shape[0]
    cap = slots // nw
    block = width // nw
    half = width // 2
    n2 = nw // 2
    bits = n2.bit_length() - 1
    chunks, _, chunk = fin.shape
    per_half = chunks // 2
    factor = 4.0 / nb
    core = lax.rem(w, 2)
    partner = w + 1 - 2 * core
    mine = w // 2

    def remote(src, dst, send, recv, dw, dk):
        return pltpu.make_async_remote_copy(
            src_ref=src, dst_ref=dst, send_sem=send, recv_sem=recv,
            device_id=(dw, dk), device_id_type=pl.DeviceIdType.MESH,
        )

    w_copy = pltpu.make_async_copy(weight_hbm, weight, local_sem.at[0])
    f_copy = pltpu.make_async_copy(feats_hbm, feats, local_sem.at[1])
    f_copy.start()
    w_copy.start()

    barrier = pltpu.get_barrier_semaphore()

    def peer_of(d):
        return lax.rem(w + d, nw)

    @pl.loop(1, nw)
    def _(d):
        pl.semaphore_signal(
            barrier, inc=1, device_id=(peer_of(d), k), device_id_type=pl.DeviceIdType.MESH
        )

    @pl.when(k > 0)
    def _():
        pl.semaphore_signal(
            barrier, inc=1, device_id=(w, k - 1), device_id_type=pl.DeviceIdType.MESH
        )

    @pl.when(k < nb - 1)
    def _():
        pl.semaphore_signal(
            barrier, inc=1, device_id=(w, k + 1), device_id_type=pl.DeviceIdType.MESH
        )

    sides = jnp.where(k > 0, 1, 0) + jnp.where(k < nb - 1, 1, 0)
    pl.semaphore_wait(barrier, nw - 1 + sides)

    def hop(src, buf, send, recv, j, step):
        side = 0 if step > 0 else 1
        return remote(src, buf.at[j], send.at[side, j], recv.at[j], w, k + step)

    def forward(src, buf, send, recv, j, step):
        @pl.when((k < nb - 1) if step > 0 else (k > 0))
        def _():
            hop(src, buf, send, recv, j, step).start()

    def begin(own, buf, send, recv):
        forward(own, buf, send, recv, k, 1)
        forward(own, buf, send, recv, k, -1)

    def coeffs(scores, labels):
        return (factor * (jax.nn.sigmoid(4.0 * scores - 2.0) - labels)).astype(BF16)

    def add_block(own, other, total):
        total[...] += dot(coeffs(rows_dot(own[...], other[...]), 0.0), other[...])

    def relay(s, buf, send, recv, own, total):
        for step in (1, -1):
            j = k - step * s

            @pl.when((j >= 0) if step > 0 else (j <= nb - 1))
            def _():
                hop(buf.at[j], buf, send, recv, j, step).wait_recv()
                forward(buf.at[j], buf, send, recv, j, step)

        for step in (1, -1):
            j = k - step * s

            @pl.when((j >= 0) if step > 0 else (j <= nb - 1))
            def _():
                add_block(own, buf.at[j], total)

    def finish(own, buf, send, recv):
        for s in range(nb):
            for step in (1, -1):
                j = k - step * s

                @pl.when(
                    ((j >= 0) & (k < nb - 1)) if step > 0 else ((j <= nb - 1) & (k > 0))
                )
                def _():
                    hop(own if s == 0 else buf.at[j], buf, send, recv, j, step).wait_send()

    begin(audio, a_buf, a_send, a_recv)

    eye = (
        lax.broadcasted_iota(jnp.int32, (rows, rows), 0)
        == lax.broadcasted_iota(jnp.int32, (rows, rows), 1)
    ).astype(F32)
    v_acc[...] = dot(coeffs(rows_dot(video[...], audio[...]), eye), audio[...])
    a_acc[...] = dot(coeffs(rows_dot(audio[...], video[...]), eye), video[...])

    scale[...] = column_of(lax.rsqrt(lengths[...].astype(F32)))
    f_copy.wait()

    @pl.loop(0, width // TILE)
    def _(t):
        cols = pl.ds(pl.multiple_of(t * TILE, TILE), TILE)
        part = (feats[:, cols].astype(F32) * scale[...]).astype(BF16)
        pooled[:, cols] = part
        pooled_t[cols, :] = part.astype(F32).T.astype(BF16)

    def pooled_copy(i):
        other = 2 * i + 1 - core
        start = pl.multiple_of(other * block, block)
        return remote(
            pooled_t.at[pl.ds(start, block), :], pooled_p.at[i],
            p_send.at[i], p_recv.at[i], partner, k,
        )

    @pl.loop(0, n2)
    def _(i):
        pooled_copy(i).start()

    w_copy.wait()

    @pl.loop(0, width // TILE)
    def _(t):
        cols = pl.ds(pl.multiple_of(t * TILE, TILE), TILE)
        v = dot(pooled[...], weight[:, cols])
        cdf = 0.5 * (1.0 + lax.erf(v * (0.5**0.5)))
        density = jnp.exp(-0.5 * v * v) * 0.3989422804014327
        gate[:, cols] = cdf + v * density

    for s in range(1, nb):
        relay(s, a_buf, a_send, a_recv, video, v_acc)
        if s == max(1, nb - 2):
            begin(video, v_buf, v_send, v_recv)

    v_grad[...] = v_acc[...].astype(BF16)
    own_row = owner[...]
    own_col = column_of(own_row)
    earlier = lax.broadcasted_iota(jnp.int32, (rows, rows), 0) < lax.broadcasted_iota(
        jnp.int32, (rows, rows), 1
    )
    same = (own_col == own_row) & earlier
    rank = jnp.sum(jnp.where(same, 1, 0), axis=0, keepdims=True)
    target = own_row * cap + rank
    placing = (
        (lax.broadcasted_iota(jnp.int32, (slots, rows), 0) == target).astype(F32).astype(BF16)
    )
    def exchange(h, peer):
        return remote(
            packed.at[h, peer], received.at[h, w], x_send.at[h, peer], x_recv.at[h, w], peer, k
        )

    for h in range(2):
        for t in range(half // TILE):
            lo = h * half + t * TILE
            placed = dot(placing, v_grad[:, lo : lo + TILE])
            packed[h, :, :, t * TILE : (t + 1) * TILE] = placed.reshape(nw, cap, TILE).astype(BF16)

        @pl.loop(1, nw)
        def _(d):
            exchange(h, peer_of(d)).start()

        received[h, w] = packed[h, w]

    def grad_copy(h):
        return remote(pre.at[h], pre_p.at[h], g_send.at[h], g_recv.at[h], partner, k)

    for h in range(2):

        @pl.loop(1, nw)
        def _(d):
            peer = peer_of(d)
            remote(
                packed.at[h, peer], received.at[h, peer], x_send.at[h, peer],
                x_recv.at[h, peer], peer, k,
            ).wait_recv()

        for t in range(half // TILE):
            lo = h * half + t * TILE
            part = slice(t * TILE, (t + 1) * TILE)
            grads = received[h, :, :, part].astype(F32).reshape(slots, TILE)
            pre[h, :, part] = (grads * gate[:, lo : lo + TILE]).astype(BF16)
        grad_copy(h).start()
        if h == 0:
            relay(1, v_buf, v_send, v_recv, audio, a_acc)

    @pl.loop(0, n2)
    def _(i):
        pooled_copy(i).wait_recv()

    def order(h):
        return list(range(bits)) if h == 0 else list(range(bits))[::-1]

    def index(h, t, flip, combo):
        taken = order(h)
        at = 0
        for place, bit in enumerate(taken):
            own = lax.rem(mine // (1 << bit), 2)
            if place < t:
                value = own
            elif place == t:
                value = 1 - own if flip else own
            else:
                value = (combo >> (place - t - 1)) & 1
            at = at + value * (1 << bit)
        return at

    def product(h, i):
        start = pl.multiple_of((2 * i + core) * block, block)
        return dot(pooled_t[pl.ds(start, block), :], pre[h]) + dot(pooled_p[i], pre_p[h])

    def scatter_copy(h, t, combo):
        bit = order(h)[t]
        sign = 1 - 2 * lax.rem(mine // (1 << bit), 2)
        peer = w + sign * (2 << bit)
        slot = n2 - (1 << (bits - t)) + combo
        return remote(
            snd.at[h, slot], rcv.at[h, slot], r_send.at[h, slot], r_recv.at[h, slot], peer, k
        )

    def combos(t):
        return range(1 << (bits - 1 - t))

    def slot_of(t, combo):
        return n2 - (1 << (bits - t)) + combo

    for h in range(2):
        grad_copy(h).wait_recv()
        for combo in combos(0):
            snd[h, slot_of(0, combo)] = product(h, index(h, 0, 1, combo)).astype(BF16)
            scatter_copy(h, 0, combo).start()
    for h in range(2):
        for combo in combos(0):
            i = index(h, 0, 0, combo)
            acc[h, i] = product(h, i)

    for s in range(2, nb - 1):
        relay(s, v_buf, v_send, v_recv, audio, a_acc)

    @pl.loop(0, width // TILE)
    def _(t):
        cols = pl.ds(pl.multiple_of(t * TILE, TILE), TILE)
        out = rows_dot(pre[0], weight[cols, :half]) + rows_dot(pre[1], weight[cols, half:])
        feats_out[:, cols] = (out * scale[...]).astype(BF16)

    def sum_copy(side, q):
        return remote(
            zs.at[side, q], zr.at[side, q], z_send.at[side, q], z_recv.at[side, q],
            w, k + 1 - 2 * side,
        )

    def scan(first, last):
        @pl.loop(first, last)
        def _(time):
            for side in range(2):
                place = k if side == 0 else nb - 1 - k
                q = time - place

                @pl.when((q >= 0) & (q < chunks))
                def _():
                    @pl.when(place > 0)
                    def _():
                        sum_copy(side, q).wait_recv()

                    @pl.when(place < nb - 1)
                    def _():
                        @pl.when(place > 0)
                        def _():
                            zs[side, q] = (fin[q] + zr[side, q].astype(F32)).astype(BF16)

                        @pl.when(place == 0)
                        def _():
                            zs[side, q] = fin[q].astype(BF16)

                        sum_copy(side, q).start()

    for t in range(bits):
        for h in range(2):
            for combo in combos(t):
                scatter_copy(h, t, combo).wait_recv()
                i = index(h, t, 0, combo)
                acc[h, i] += rcv[h, slot_of(t, combo)].astype(F32)
            if t + 1 < bits:
                for combo in combos(t + 1):
                    i = index(h, t + 1, 1, combo)
                    snd[h, slot_of(t + 1, combo)] = acc[h, i].astype(BF16)
                    scatter_copy(h, t + 1, combo).start()
            else:
                for q in range(per_half):
                    fin[h * per_half + q] = acc[h, mine, :, q * chunk : (q + 1) * chunk]
                if h == 0:
                    scan(0, per_half)
        if t == 0:
            for s in range(max(2, nb - 1), nb):
                relay(s, v_buf, v_send, v_recv, audio, a_acc)
            audio_out[...] = a_acc[...].astype(BF16)
    scan(per_half, nb - 1 + chunks)

    for q in range(chunks):
        cols = slice(q * chunk, (q + 1) * chunk)
        weight_out[:, cols] = fin[q]

        @pl.when(k > 0)
        def _():
            weight_out[:, cols] += zr[0, q].astype(F32)

        @pl.when(k < nb - 1)
        def _():
            weight_out[:, cols] += zr[1, q].astype(F32)

    finish(audio, a_buf, a_send, a_recv)
    finish(video, v_buf, v_send, v_recv)

    @pl.loop(0, n2)
    def _(i):
        pooled_copy(i).wait_send()

    @pl.loop(1, nw)
    def _(d):
        for h in range(2):
            exchange(h, peer_of(d)).wait_send()

    for h in range(2):
        grad_copy(h).wait_send()
        for t in range(bits):
            for combo in combos(t):
                scatter_copy(h, t, combo).wait_send()

    @pl.loop(0, chunks)
    def _(q):
        @pl.when(k < nb - 1)
        def _():
            sum_copy(0, q).wait_send()

        @pl.when(k > 0)
        def _():
            sum_copy(1, q).wait_send()


def store(*refs):
    sems = refs[6]
    copies = [pltpu.make_async_copy(refs[i], refs[3 + i], sems.at[i]) for i in range(3)]
    for copy in copies:
        copy.start()
    for copy in copies:
        copy.wait()


def shards(nw, nb, audio, video, owner, clip_feats, lengths, proj_weight):
    rows, width = audio.shape
    slots = clip_feats.shape[0]
    cap, block, half, n2 = slots // nw, width // nw, width // 2, nw // 2
    chunks = 2 * SPLIT
    chunk = width // chunks
    vmem = pl.BlockSpec(memory_space=pltpu.VMEM)
    hbm = pl.BlockSpec(memory_space=pl.ANY)
    dma = pltpu.SemaphoreType.DMA
    outs = pl.pallas_call(
        functools.partial(kernel, nw, nb),
        out_shape=(
            pltpu.VMEM((rows, width), BF16),
            pltpu.VMEM((slots, width), BF16),
            pltpu.VMEM((block, width), F32),
        ),
        in_specs=[vmem, vmem, vmem, vmem, hbm, hbm],
        out_specs=(vmem, vmem, vmem),
        scratch_shapes=[
            pltpu.VMEM((slots, width), BF16),
            pltpu.VMEM(proj_weight.shape, BF16),
            pltpu.VMEM((nb, rows, width), BF16),
            pltpu.VMEM((nb, rows, width), BF16),
            pltpu.VMEM((rows, width), F32),
            pltpu.VMEM((rows, width), F32),
            pltpu.VMEM((rows, width), BF16),
            pltpu.VMEM((slots, 1), F32),
            pltpu.VMEM((slots, width), BF16),
            pltpu.VMEM((width, slots), BF16),
            pltpu.VMEM((n2, block, slots), BF16),
            pltpu.VMEM((slots, width), F32),
            pltpu.VMEM((2, nw, cap, half), BF16),
            pltpu.VMEM((2, nw, cap, half), BF16),
            pltpu.VMEM((2, slots, half), BF16),
            pltpu.VMEM((2, slots, half), BF16),
            pltpu.VMEM((2, n2, block, half), F32),
            pltpu.VMEM((2, n2, block, half), BF16),
            pltpu.VMEM((2, n2, block, half), BF16),
            pltpu.VMEM((chunks, block, chunk), F32),
            pltpu.VMEM((2, chunks, block, chunk), BF16),
            pltpu.VMEM((2, chunks, block, chunk), BF16),
            dma((2,)),
            dma((2, nb)), dma((nb,)),
            dma((2, nb)), dma((nb,)),
            dma((n2,)), dma((n2,)),
            dma((2, nw)), dma((2, nw)),
            dma((2,)), dma((2,)),
            dma((2, n2)), dma((2, n2)),
            dma((2, chunks)), dma((2, chunks)),
        ],
        compiler_params=pltpu.CompilerParams(
            collective_id=0, has_side_effects=True, vmem_limit_bytes=60 * 1024 * 1024
        ),
    )(
        audio, video, owner.reshape(1, rows), lengths.reshape(1, slots), clip_feats, proj_weight
    )
    return pl.pallas_call(
        store,
        out_shape=tuple(jax.ShapeDtypeStruct(out.shape, out.dtype) for out in outs),
        in_specs=[vmem, vmem, vmem],
        out_specs=(hbm, hbm, hbm),
        scratch_shapes=[dma((3,))],
    )(*[pltpu.with_memory_space_constraint(out, pltpu.VMEM) for out in outs])


def solution(mesh):
    return jax.shard_map(
        functools.partial(shards, mesh.shape["wide"], mesh.shape["blk"]),
        mesh=mesh,
        in_specs=(
            P(("wide", "blk"), None),
            P(("wide", "blk"), None),
            P(("wide", "blk"), None),
            P(("wide", "blk"), None),
            P(("wide", "blk")),
            P(),
        ),
        out_specs=(P(("wide", "blk"), None), P(("wide", "blk"), None), P("wide", None)),
        check_vma=False,
    )
```
